32 devices in a mesh: inst: 4 (over z), shard: 8 (over y, x, core).
Axes of the slice: x: 2, y: 2, z: 4, core: 2. Of those that a mesh axis runs over, the one named last changes fastest.
Arguments:
- master_old: float32 [4, 16, 65536], P('inst', 'shard'), may hold values from -3 to 3
- first_old: float32 [4, 16, 65536], P('inst', 'shard'), may hold values from -2 to 2
- second_old: float32 [4, 16, 65536], P('inst', 'shard'), may hold values from 0.01 to 1
- healthy: int32 [8], replicated, may hold values from 0 to 3
- slice_table: int32 [16], replicated, may hold values from 0 to 15, as said below
Outputs:
- master_new: float32 [4, 16, 65536], P('inst', 'shard')
- first_new: float32 [4, 16, 65536], P('inst', 'shard')
- second_new: float32 [4, 16, 65536], P('inst', 'shard')
- params_half: bfloat16 [4, 16, 65536], P('inst', 'shard')
- checksum: float32 [4, 2], P('inst')
The draws below stay inside these ranges and needn't reach their ends.
Inputs may be any that keep to these rules, and one draw needn't show every extreme that they name: slice_table[k] = (k + slice_table[0]) mod 16 for every k, with slice_table[0] odd and at least 3.
All inputs are finite; a program needn't handle non-finite values.
Results may differ from the reference program's by a relative error of at most 0.001.
Values sent between devices are 32-bit elements; how exact they have to be, the bound alone decides.
No kernel may reach another device: no remote copies, remote signals or barrier semaphores. Data moves between devices by JAX's collectives and lax.ppermute only.
A program may use at most 64 MiB of HBM per device.

```python
import math
import jax
import jax.numpy as jnp

SLICE = 65536
OLD = 16
N_INST = 4
N_SHARD = 8


def draw_slice_table(key, part):
    rotation = 2 * jax.random.randint(jax.random.fold_in(key, 11), (), 1, OLD // 2) + 1
    return ((jnp.arange(OLD, dtype=jnp.int32) + rotation) % OLD).astype(jnp.int32)


def with_ends(array, key, least, high):
    shape = array.shape
    spot = [jax.random.randint(jax.random.fold_in(key, axis), (), 0, shape[axis]) for axis in range(len(shape))]
    array = array.at[tuple(spot)].set(least)
    longest = shape.index(max(shape))
    spot[longest] = (spot[longest] + 1) % shape[longest]
    return array.at[tuple(spot)].set(high)


def block_scale(stream_key, shape, pieces, least, largest):
    def one(dim, parts):
        heights = jax.random.uniform(jax.random.fold_in(jax.random.fold_in(stream_key, 6), dim), (parts,), jnp.float32, least / len(pieces), largest / len(pieces))
        return jnp.repeat(jnp.exp(heights), shape[dim] // parts).reshape((-1,) + (1,) * (len(shape) - dim - 1))

    gain = one(*pieces[0])
    for cut in pieces[1:]:
        gain = gain * one(*cut)
    return gain


def centred(key, extent, width, reach, shards=(), kind=jnp.bfloat16):
    drawn = width * jax.random.normal(key, extent, jnp.float32)
    if shards:
        drawn = drawn * block_scale(key, extent, shards, -0.22, 0.18)
    return jnp.clip(drawn, -reach, reach).astype(kind)


def setup_inputs(seed: int = 0) -> dict:
    key_of = jax.random.split(jax.random.key(seed), 6)
    return {
        "master_old": centred(key_of[0], (N_INST, OLD, SLICE), 0.5, 3.0, ((0, 4), (1, 8)), jnp.float32),
        "first_old": centred(key_of[1], (N_INST, OLD, SLICE), 0.3, 2.0, ((0, 4), (1, 8)), jnp.float32),
        "second_old": jnp.clip(jnp.exp(math.log(1.0) - 4.6051702 * jax.random.uniform(key_of[2], (N_INST, OLD, SLICE), jnp.float32) ** block_scale(key_of[2], (N_INST, OLD, SLICE), ((0, 4), (1, 8)), -0.2, 0.2)), 0.01, 1.0),
        "healthy": with_ends(jax.random.randint(key_of[3], (N_SHARD,), 0, N_INST), jax.random.fold_in(key_of[3], 1), 0, N_INST - 1).astype(jnp.int32),
        "slice_table": draw_slice_table(jax.random.fold_in(key_of[5], 71), 0),
    }


def position_keys(flat_rows, columns):
    residue = (flat_rows.astype(jnp.int32) * (columns % 101)) % 101
    offsets = jnp.arange(columns, dtype=jnp.int32)
    cycled = (residue[:, None] + offsets[None, :]) % 101
    return ((cycled * 37) % 101 + 1).astype(jnp.float32) / 101.0


def reference(master_old, first_old, second_old, healthy, slice_table):
    inverse = jnp.zeros((OLD,), jnp.int32).at[slice_table].set(jnp.arange(OLD, dtype=jnp.int32))
    row_source = jnp.repeat(healthy.astype(jnp.int32), 2)
    row_index = jnp.arange(OLD, dtype=jnp.int32)

    def select_rows(stacked):
        source = stacked[row_source, row_index]
        return jnp.take(source, inverse, axis=0)

    master = select_rows(master_old)
    first_moment = select_rows(first_old)
    second = select_rows(second_old)
    combined = master + first_moment + second
    weights = position_keys(jnp.arange(OLD, dtype=jnp.int32), SLICE)
    scale = jnp.float32(2 * SLICE)
    total_all = jnp.sum(combined * weights) / scale
    total_master = jnp.sum(master * weights) / scale
    sums = jnp.stack([total_all, total_master]).astype(jnp.float32)

    def replicate(stacked):
        return jnp.broadcast_to(stacked[None], (N_INST,) + stacked.shape)

    return (replicate(master), replicate(first_moment), replicate(second),
            replicate(master.astype(jnp.bfloat16)), replicate(sums))
```

```python
import functools

import jax
import jax.numpy as jnp
from jax import lax
from jax.experimental import pallas as pl
from jax.experimental.pallas import tpu as pltpu
from jax.sharding import PartitionSpec as P


LINES = ("inst", "shard")
LANES = 128
SUBLANES = 8
PERIOD = 101
FACTOR = 37
WIDTH = 8


def tiled(stacked):
    columns = stacked.shape[2]
    return stacked.reshape(2, columns // LANES, LANES).transpose(1, 0, 2).reshape(2 * columns // LANES, LANES)


def untiled(flat):
    height = flat.shape[0]
    return flat.reshape(height // 2, 2, LANES).transpose(1, 0, 2).reshape(1, 2, height // 2 * LANES)


def split_kernel(columns, table, healthy, master, first, second, *outs):
    own, sums = outs[:6], outs[6]
    shard = lax.axis_index("shard")
    height = columns // LANES
    stride = SUBLANES * LANES
    present = healthy[shard] == lax.axis_index("inst")
    scale = jnp.where(present, 1.0, 0.0) / (2.0 * columns * PERIOD)
    place = (lax.broadcasted_iota(jnp.int32, (SUBLANES, LANES), 0) * LANES
             + lax.broadcasted_iota(jnp.int32, (SUBLANES, LANES), 1)) % PERIOD
    jump = float(FACTOR * (stride % PERIOD) % PERIOD)
    total = jnp.zeros((SUBLANES, LANES), jnp.float32)
    alone = jnp.zeros((SUBLANES, LANES), jnp.float32)
    for row in range(2):
        residue = table[2 * shard + row] * (columns % PERIOD) % PERIOD
        key = ((place + residue) % PERIOD * FACTOR % PERIOD + 1).astype(jnp.float32)

        def step(block, carry):
            key, total, alone = carry
            here = pl.ds(block * 2 * SUBLANES + row, SUBLANES, stride=2)
            there = pl.ds(block * SUBLANES, SUBLANES)
            m, f, s = master[here, :], first[here, :], second[here, :]
            own[row][there, :] = m
            own[2 + row][there, :] = f
            own[4 + row][there, :] = s
            total = total + (m + f + s) * key
            alone = alone + m * key
            key = key + jump
            return jnp.where(key > float(PERIOD), key - float(PERIOD), key), total, alone

        _, total, alone = lax.fori_loop(0, height // SUBLANES, step, (key, total, alone), unroll=4)
    sums[0:SUBLANES, :] = jnp.broadcast_to(jnp.sum(total) * scale, (SUBLANES, LANES))
    sums[SUBLANES:, :] = jnp.broadcast_to(jnp.sum(alone) * scale, (SUBLANES, LANES))


def split(arrays, table, healthy):
    columns = arrays[0].shape[2]
    height = columns // LANES
    piece = jax.ShapeDtypeStruct((height, LANES), jnp.float32)
    smem = pl.BlockSpec(memory_space=pltpu.SMEM)
    vmem = pl.BlockSpec(memory_space=pltpu.VMEM)
    outs = pl.pallas_call(
        functools.partial(split_kernel, columns),
        out_shape=[piece] * 6 + [jax.ShapeDtypeStruct((2 * SUBLANES, LANES), jnp.float32)],
        in_specs=[smem, smem, vmem, vmem, vmem],
        out_specs=[vmem] * 7,
        compiler_params=pltpu.CompilerParams(vmem_limit_bytes=8 * 1024 * 1024),
        name="split",
    )(table, healthy, *[tiled(a) for a in arrays])
    return outs[:6], outs[6]


def join_kernel(*refs):
    ins, outs = refs[:12], refs[12:]
    inst = lax.axis_index("inst")
    outer = (inst == 0) | (inst == lax.axis_size("inst") - 1)

    def fill(side):
        for array in range(3):
            height = ins[0].shape[0]

            def step(block, _):
                there = pl.ds(block * SUBLANES, SUBLANES)
                for row in range(2):
                    value = ins[side * 6 + array * 2 + 1 - row][there, :]
                    outs[array][pl.ds(block * 2 * SUBLANES + row, SUBLANES, stride=2), :] = value
                if array == 0:
                    whole = pl.ds(block * 2 * SUBLANES, 2 * SUBLANES)
                    outs[3][whole, :] = outs[0][whole, :].astype(jnp.bfloat16)
                return 0

            lax.fori_loop(0, height // SUBLANES, step, 0, unroll=4)

    pl.when(outer)(lambda: fill(0))
    pl.when(jnp.logical_not(outer))(lambda: fill(1))


def join(edge, here):
    height = edge[0].shape[0]
    vmem = pl.BlockSpec(memory_space=pltpu.VMEM)
    outs = pl.pallas_call(
        join_kernel,
        out_shape=[jax.ShapeDtypeStruct((2 * height, LANES), jnp.float32)] * 3
        + [jax.ShapeDtypeStruct((2 * height, LANES), jnp.bfloat16)],
        in_specs=[vmem] * 12,
        out_specs=[vmem] * 4,
        compiler_params=pltpu.CompilerParams(vmem_limit_bytes=8 * 1024 * 1024),
        name="join",
    )(*edge, *here)
    return tuple(untiled(v) for v in outs)


def hop(value, pairs):
    return lax.ppermute(value, LINES, pairs)


def restore(own, sums, source, instances, owners, turn):
    inst = lax.axis_index("inst")
    last = instances - 1
    mid = instances // 2

    def pairs(moves, filler=()):
        out = [(a * owners + s, b * owners + (s + d) % owners) for a, b, d in moves for s in range(owners)]
        return out + [(a * owners + s, a * owners + (s ^ 1)) for a in filler for s in range(owners)]

    across = pairs([(1, 2, 0), (2, 1, 0)], (0, 3))

    def turned(d):
        return pairs([(1, 1, d), (2, 2, d)], (0, 3))

    def shuttle(d):
        return pairs([(0, 1, 0), (3, 2, 0), (1, 0, d), (2, 3, d)])

    outer = (inst == 0) | (inst == last)
    mine_here = source == inst
    same_half = (source < mid) == (inst < mid)

    steps = [(1 << b, "shard", owners) for b in range((owners - 1).bit_length())]
    steps += [(1 << b, "inst", instances) for b in range((instances - 1).bit_length())]

    count = len(own)
    lag = 3
    got, far, near, full, edge, here = {}, {}, {}, {}, {}, {}

    def send_shuttle(t):
        cargo = own[min(t, count - 1)]
        shift = 0
        if t >= lag:
            cargo = jnp.where(outer, cargo, full[t - lag]) if t < count else full[t - lag]
            shift = turn + (t - lag) % 2
        back = hop(cargo, shuttle(shift))
        if t < count:
            got[t] = back
        if t >= lag:
            edge[t - lag] = back

    def tick(anchor):
        nonlocal sums
        if steps:
            step, axis, size = steps.pop(0)
            tied, _ = lax.optimization_barrier((sums, anchor))
            sums = tied + lax.ppermute(tied, axis, [(s, s ^ step) for s in range(size)])

    send_shuttle(0)
    send_shuttle(1)
    for t in range(count + 1):
        if t < count:
            near[t] = jnp.where(mine_here, own[t], got[t])
            far[t] = hop(near[t], across)
        if t >= 1:
            full[t - 1] = jnp.where(same_half, near[t - 1], far[t - 1])
        if t + 2 < count or t >= 1:
            send_shuttle(t + 2)
        if t >= 1:
            here[t - 1] = hop(full[t - 1], turned(turn + (t - 1) % 2))
        tick(near[t] if t < count else full[t - 1])
    while steps:
        tick(full[count - 1])
    return [edge[c] for c in range(count)], [here[c] for c in range(count)], sums


def on_device(master_old, first_old, second_old, healthy, slice_table):
    shard = lax.axis_index("shard")
    owners = lax.axis_size("shard")
    instances = lax.axis_size("inst")
    arrays = (master_old, first_old, second_old)
    turn = slice_table[0] // 2
    own, sums = split(arrays, slice_table, healthy)
    width = min(owners, WIDTH)
    step = width
    while step < owners:
        chosen = turn // step % 2 == 1
        moved = [lax.ppermute(v, "shard", [(s, (s + step) % owners) for s in range(owners)]) for v in own]
        own = [jnp.where(chosen, m, v) for m, v in zip(moved, own)]
        step *= 2
    begin = (shard - turn // width * width) % owners
    source = lax.dynamic_index_in_dim(healthy, begin, 0, keepdims=False)
    lowest = 1 if width == owners else 0

    def branch(turned_by):
        def run(pieces, terms, origin):
            return restore(pieces, terms, origin, instances, owners, turned_by)

        return run

    branches = [branch(t) for t in range(lowest, width)]
    edge, here, sums = lax.switch(turn % width - lowest, branches, own, sums, source)
    checksum = sums[::SUBLANES, 0].reshape(1, 2)
    return (*join(edge, here), checksum)


def solution(mesh):
    placed = (
        P("inst", "shard", None),
        P("inst", "shard", None),
        P("inst", "shard", None),
        P(),
        P(),
    )
    return jax.shard_map(
        on_device,
        mesh=mesh,
        in_specs=placed,
        out_specs=(
            P("inst", "shard", None),
            P("inst", "shard", None),
            P("inst", "shard", None),
            P("inst", "shard", None),
            P("inst", None),
        ),
        check_vma=False,
    )
```
